512 devices in a mesh: row: 64 (over z, y), col: 8 (over x, core).
Axes of the slice: x: 4, y: 8, z: 8, core: 2. Of those that a mesh axis runs over, the one named last changes fastest.
Arguments:
- frames: bfloat16 [4, 16384, 8192], P(None, 'row', 'col'), may hold values from -6 to 6
- row_factor: bfloat16 [16384, 256], P('row')
- col_factor: bfloat16 [8192, 256], P('col')
- row_history: float32 [16384, 256], P('row'), may hold values from -8 to 8
- col_history: float32 [8192, 256], P('col'), may hold values from -8 to 8
- time_gram: float32 [256, 256], replicated, as said below
Outputs:
- frame_factor: float32 [4, 256], replicated
- new_row_factor: bfloat16 [16384, 256], P('row')
- new_col_factor: bfloat16 [8192, 256], P('col')
The draws below stay inside these ranges and needn't reach their ends.
Inputs may be any that keep to these rules, and one draw needn't show every extreme that they name: `time_gram`: symmetric positive definite.
All inputs are finite; a program needn't handle non-finite values.
Results may differ from the reference program's by a relative error of at most 0.0041.
Values may be sent and summed in bfloat16 or wider, within the bound.
No kernel may reach another device: no remote copies, remote signals or barrier semaphores. Data moves between devices by JAX's collectives and lax.ppermute only.
A program may use at most 64 MiB of HBM per device.

```python
import math
import jax
import jax.numpy as jnp
from jax import lax

R = 256
NB = 4
ROWS = 16384
COLS = 8192


def factor_draw(key, count):
    key_noise, key_common = jax.random.split(key, 2)
    noise = jnp.clip(jax.random.normal(key_noise, (count, R), jnp.float32), -5.0, 5.0)
    common = jnp.clip(jax.random.normal(key_common, (count, 1), jnp.float32), -5.0, 5.0)
    return (noise + 0.7 * common) / math.sqrt(count)


def draw_row_factor(key, part):
    return factor_draw(jax.random.fold_in(key, 11), ROWS).astype(jnp.bfloat16)


def draw_col_factor(key, part):
    return factor_draw(jax.random.fold_in(key, 23), COLS).astype(jnp.bfloat16)


def draw_time_gram(key, part):
    key_off, key_diag = jax.random.split(jax.random.fold_in(key, 37))
    offdiag = jax.random.uniform(key_off, (R, R), jnp.float32, -0.01, 0.01)
    offdiag = 0.5 * (offdiag + offdiag.T)
    diag_vals = jax.random.uniform(key_diag, (R,), jnp.float32, 3.0, 4.0)
    identity = jnp.eye(R, dtype=jnp.float32)
    return offdiag * (1.0 - identity) + identity * diag_vals[None, :]


def steps_of(stream_key, extent, shards, low, high):
    def one(dim, parts):
        steps = jax.random.uniform(jax.random.fold_in(jax.random.fold_in(stream_key, 6), dim), (parts,), jnp.float32, low / len(shards), high / len(shards))
        return jnp.repeat(jnp.exp(steps), extent[dim] // parts).reshape((-1,) + (1,) * (len(extent) - dim - 1))

    loudness = one(*shards[0])
    for cut in shards[1:]:
        loudness = loudness * one(*cut)
    return loudness


def gaussian(stream_key, dims, spread, limit, cuts=(), kind=jnp.bfloat16):
    result = spread * jax.random.normal(stream_key, dims, jnp.float32)
    if cuts:
        result = result * steps_of(stream_key, dims, cuts, -0.22, 0.18)
    return jnp.clip(result, -limit, limit).astype(kind)


def setup_inputs(seed: int = 0) -> dict:
    key_list = jax.random.split(jax.random.key(seed), 7)
    frames = gaussian(key_list[0], (NB, ROWS, COLS), 1.0, 6.0, ((1, 64), (2, 8)))
    row_factor = draw_row_factor(jax.random.fold_in(key_list[6], 71), 0)
    col_factor = draw_col_factor(jax.random.fold_in(key_list[6], 71), 0)
    row_history = gaussian(key_list[3], (ROWS, R), 2.0, 8.0, ((0, 64),), jnp.float32)
    col_history = gaussian(key_list[4], (COLS, R), 2.0, 8.0, ((0, 8),), jnp.float32)
    time_gram = draw_time_gram(jax.random.fold_in(key_list[6], 71), 0)
    return {"frames": frames, "row_factor": row_factor, "col_factor": col_factor, "row_history": row_history, "col_history": col_history, "time_gram": time_gram}


def inner_gram(matrix):
    return lax.dot_general(matrix.astype(jnp.float32), matrix.astype(jnp.float32), (((0,), (0,)), ((), ())), preferred_element_type=jnp.float32)

def gram_solve(rhs, gram):
    lower_factor = jnp.linalg.cholesky(gram)
    return jax.scipy.linalg.cho_solve((lower_factor, True), rhs.T).T

def reference(frames, row_factor, col_factor, row_history, col_history, time_gram):
    row_gram = inner_gram(row_factor)
    col_gram = inner_gram(col_factor)

    def slab_one(frame):
        return jnp.dot(frame.astype(jnp.float32), col_factor.astype(jnp.float32), preferred_element_type=jnp.float32)
    slab_products = lax.map(slab_one, frames)
    frame_rhs = jnp.sum(slab_products * row_factor.astype(jnp.float32)[None], axis=1)
    frame_factor = gram_solve(frame_rhs, row_gram * col_gram)
    time_new = time_gram + jnp.dot(frame_factor.T, frame_factor, precision=lax.Precision.HIGHEST)
    row_sums = row_history + jnp.sum(frame_factor[:, None, :] * slab_products, axis=0)
    new_row = gram_solve(row_sums, time_new * col_gram).astype(jnp.bfloat16)
    new_row_gram = inner_gram(new_row)

    def column_one(frame):
        return lax.dot_general(frame.astype(jnp.float32), new_row.astype(jnp.float32), (((0,), (0,)), ((), ())), preferred_element_type=jnp.float32)
    col_prods = lax.map(column_one, frames)
    col_sums = col_history + jnp.sum(frame_factor[:, None, :] * col_prods, axis=0)
    new_col = gram_solve(col_sums, time_new * new_row_gram).astype(jnp.bfloat16)
    return (frame_factor, new_row, new_col)
```

```python
import jax
import jax.numpy as jnp
from jax import lax
from jax.experimental import pallas as pl
from jax.experimental.pallas import tpu as pltpu
from jax.sharding import PartitionSpec as P

R = 256
HALF = 128
HIGHEST = lax.Precision.HIGHEST
F32 = jnp.float32


def inner_gram(matrix):
    return lax.dot_general(
        matrix, matrix, (((0,), (0,)), ((), ())), preferred_element_type=F32
    )


def matmul_f32(a, b, dims=((1,), (0,))):
    return lax.dot_general(a, b, (dims, ((), ())), precision=HIGHEST, preferred_element_type=F32)


def eliminate8(tile, g):
    lane = lax.broadcasted_iota(jnp.int32, (8, R), 1)
    cols = [jnp.broadcast_to(tile[:, g + j : g + j + 1], (8, HALF)) for j in range(8)]
    s = {}
    for j in range(8):
        for i in range(j, 8):
            s[i, j] = s[j, i] = jnp.broadcast_to(cols[j][i : i + 1, :], (8, HALF))
    inside = (lane >= g) & (lane < g + 8)
    rows = []
    for i in range(8):
        row = jnp.broadcast_to(tile[i : i + 1, :], (8, R))
        rows.append(jnp.where(inside, jnp.where(lane == g + i, 1.0, 0.0), row))
    for k in range(8):
        inv = 1.0 / s[k, k]
        p = {j: s[k, j] * inv for j in range(k + 1, 8)}
        rows[k] = rows[k] * jnp.concatenate([inv, inv], 1)
        new = {}
        for j in range(k + 1, 8):
            for i in range(8):
                if i == k or k < i < j:
                    continue
                new[i, j] = s[i, j] - s[i, k] * p[j]
        for i in range(8):
            if i != k:
                rows[i] = rows[i] - jnp.concatenate([s[i, k]] * 2, 1) * rows[k]
        for (i, j), v in new.items():
            s[i, j] = v
            if i > k:
                s[j, i] = v
        for j in range(k + 1, 8):
            s[k, j] = p[j]
    return rows


def spd_inverse(a):
    lane8 = lax.broadcasted_iota(jnp.int32, (8, R), 1)
    sub8 = lax.broadcasted_iota(jnp.int32, (8, R), 0)
    groups = HALF // 8
    for start in (0, HALF):
        tiles = [a[start + 8 * m : start + 8 * m + 8, :] for m in range(groups)]
        for b in range(groups):
            g = start + 8 * b
            rows = eliminate8(tiles[b], g)
            inside = (lane8 >= g) & (lane8 < g + 8)
            for m in list(range(b + 1, groups)) + list(range(b)):
                acc = [
                    jnp.broadcast_to(tiles[m][:, g + j : g + j + 1], (8, R)) * rows[j]
                    for j in range(8)
                ]
                while len(acc) > 1:
                    acc = [acc[i] + acc[i + 1] for i in range(0, len(acc), 2)]
                tiles[m] = jnp.where(inside, 0.0, tiles[m]) - acc[0]
            merged = rows[0]
            for j in range(1, 8):
                merged = jnp.where(sub8 == j, rows[j], merged)
            tiles[b] = merged
        panel = jnp.concatenate(tiles, 0)
        other = HALF - start
        rest = a[other : other + HALF, :]
        update = matmul_f32(rest[:, start : start + HALF], panel)
        lane = lax.broadcasted_iota(jnp.int32, (HALF, R), 1)
        inside = (lane >= start) & (lane < start + HALF)
        rest = jnp.where(inside, 0.0, rest) - update
        a = jnp.concatenate([panel, rest] if start == 0 else [rest, panel], 0)
    return a


def time_kernel(row_gram, col_gram, rhs, time_gram, factor_out, time_out, inverse_out):
    factor = matmul_f32(rhs[...], spd_inverse(row_gram[...] * col_gram[...]))
    factor_out[...] = factor
    time_new = time_gram[...] + matmul_f32(factor, factor, ((0,), (0,)))
    time_out[...] = time_new
    inverse_out[...] = spd_inverse(time_new * col_gram[...])


def col_kernel(time_new, gram, sums, out):
    inverse = spd_inverse(time_new[...] * gram[...])
    out[...] = matmul_f32(sums[...], inverse).astype(out.dtype)


def gather(x, axis, count):
    return lax.all_to_all(jnp.broadcast_to(x[None], (count,) + x.shape), axis, 0, 0)


def body(frames, row_factor, col_factor, row_history, col_history, time_gram):
    nrow = lax.axis_size("row")
    ncol = lax.axis_size("col")
    r = lax.axis_index("row")
    own = R // nrow
    row_part = inner_gram(row_factor)
    col_part = inner_gram(col_factor)
    slab_part = jnp.einsum("bij,jr->bir", frames, col_factor, preferred_element_type=F32)
    rhs_part = jnp.sum(slab_part * row_factor.astype(F32)[None], axis=1)
    slab_own = lax.psum_scatter(slab_part, "col", scatter_dimension=1, tiled=True)
    slab = lax.all_gather(slab_own, "col", axis=1, tiled=True)

    col_piece = lax.dynamic_slice_in_dim(col_part, own * r, own, 0)
    first = gather(jnp.concatenate([col_piece, rhs_part], 0), "col", ncol).sum(0)
    col_piece, rhs_part = first[:own], first[own:]

    nb = rhs_part.shape[0]
    rhs_pad = jnp.pad(
        rhs_part.reshape(nb, nrow, own).transpose(1, 0, 2), ((0, 0), (0, 0), (0, HALF - own))
    )
    second = jnp.concatenate([row_part.reshape(nrow, own, R), rhs_pad], 2)
    second = lax.all_to_all(second, "row", 0, 0).sum(0)
    third = gather(jnp.concatenate([second, col_piece], 1), "row", nrow)
    row_gram = third[:, :, :R].reshape(R, R)
    col_gram = third[:, :, R + HALF :].reshape(R, R)
    rhs = third[:, :, R : R + own].transpose(1, 0, 2).reshape(nb, R)

    square = jax.ShapeDtypeStruct((R, R), F32)
    frame_factor, time_new, inverse = pl.pallas_call(
        time_kernel,
        out_shape=(jax.ShapeDtypeStruct((nb, R), F32), square, square),
        name="time_solve",
    )(row_gram, col_gram, rhs, time_gram)

    row_sums = row_history + jnp.sum(frame_factor[:, None, :] * slab, axis=0)
    new_row = matmul_f32(row_sums, inverse).astype(jnp.bfloat16)
    gram_part = inner_gram(new_row)
    products = jnp.einsum("bij,ir->bjr", frames, new_row, preferred_element_type=F32)
    col_part = jnp.sum(frame_factor[:, None, :] * products, axis=0)
    high = gram_part.astype(jnp.bfloat16)
    low = (gram_part - high.astype(F32)).astype(jnp.bfloat16)
    chunk = col_part.shape[0] // nrow
    message = jnp.concatenate(
        [
            col_part.astype(jnp.bfloat16).reshape(nrow, chunk, R),
            high.reshape(nrow, own, R),
            low.reshape(nrow, own, R),
        ],
        1,
    )
    total = lax.all_to_all(message, "row", 0, 0).astype(F32).sum(0)
    gram_own = total[chunk : chunk + own] + total[chunk + own :]
    new_gram = gather(gram_own, "row", nrow).reshape(R, R)
    col_sums = lax.dynamic_slice_in_dim(col_history, chunk * r, chunk, 0) + total[:chunk]
    new_col_own = pl.pallas_call(
        col_kernel,
        out_shape=jax.ShapeDtypeStruct((chunk, R), jnp.bfloat16),
        name="col_solve",
    )(time_new, new_gram, col_sums)
    new_col = gather(new_col_own, "row", nrow).reshape(nrow * chunk, R)
    return (frame_factor, new_row, new_col)


def solution(mesh):
    in_specs = (
        P(None, "row", "col"),
        P("row", None),
        P("col", None),
        P("row", None),
        P("col", None),
        P(),
    )
    out_specs = (P(), P("row", None), P("col", None))
    return jax.shard_map(body, mesh=mesh, in_specs=in_specs, out_specs=out_specs, check_vma=False)
```

```python
import jax
import jax.numpy as jnp
from jax import lax
from jax.experimental import pallas as pl
from jax.experimental.pallas import tpu as pltpu
from jax.sharding import PartitionSpec as P

R = 256
HALF = 128
HIGHEST = lax.Precision.HIGHEST
F32 = jnp.float32


def inner_gram(matrix):
    return lax.dot_general(
        matrix, matrix, (((0,), (0,)), ((), ())), preferred_element_type=F32
    )


def matmul_f32(a, b, dims=((1,), (0,))):
    return lax.dot_general(a, b, (dims, ((), ())), precision=HIGHEST, preferred_element_type=F32)


def eliminate8(tile, g):
    lane = lax.broadcasted_iota(jnp.int32, (8, R), 1)
    cols = [jnp.broadcast_to(tile[:, g + j : g + j + 1], (8, HALF)) for j in range(8)]
    s = {}
    for j in range(8):
        for i in range(j, 8):
            s[i, j] = s[j, i] = jnp.broadcast_to(cols[j][i : i + 1, :], (8, HALF))
    inside = (lane >= g) & (lane < g + 8)
    rows = []
    for i in range(8):
        row = jnp.broadcast_to(tile[i : i + 1, :], (8, R))
        rows.append(jnp.where(inside, jnp.where(lane == g + i, 1.0, 0.0), row))
    for k in range(8):
        inv = pl.reciprocal(s[k, k])
        p = {j: s[k, j] * inv for j in range(k + 1, 8)}
        rows[k] = rows[k] * jnp.concatenate([inv, inv], 1)
        new = {}
        for j in range(k + 1, 8):
            for i in range(8):
                if i == k or k < i < j:
                    continue
                new[i, j] = s[i, j] - s[i, k] * p[j]
        for i in range(8):
            if i != k:
                rows[i] = rows[i] - jnp.concatenate([s[i, k]] * 2, 1) * rows[k]
        for (i, j), v in new.items():
            s[i, j] = v
            if i > k:
                s[j, i] = v
        for j in range(k + 1, 8):
            s[k, j] = p[j]
    return rows


def half_inverse(m):
    lane8 = lax.broadcasted_iota(jnp.int32, (8, R), 1)
    sub8 = lax.broadcasted_iota(jnp.int32, (8, R), 0)
    groups = HALF // 8
    tiles = [m[8 * i : 8 * i + 8, :] for i in range(groups)]
    for b in range(groups):
        g = 8 * b
        rows = eliminate8(tiles[b], g)
        inside = (lane8 >= g) & (lane8 < g + 8)
        for i in list(range(b + 1, groups)) + list(range(b)):
            acc = [
                jnp.broadcast_to(tiles[i][:, g + j : g + j + 1], (8, R)) * rows[j]
                for j in range(8)
            ]
            while len(acc) > 1:
                acc = [acc[k] + acc[k + 1] for k in range(0, len(acc), 2)]
            tiles[i] = jnp.where(inside, 0.0, tiles[i]) - acc[0]
        merged = rows[0]
        for j in range(1, 8):
            merged = jnp.where(sub8 == j, rows[j], merged)
        tiles[b] = merged
    panel = jnp.concatenate(tiles, 0)
    rest = m[HALF:, :]
    update = matmul_f32(rest[:, :HALF], panel)
    m[:HALF, :HALF] = rest[:, HALF:] - update[:, HALF:]
    m[:HALF, HALF:] = -update[:, :HALF]
    m[HALF:, :HALF] = panel[:, HALF:]
    m[HALF:, HALF:] = panel[:, :HALF]


def square_iota():
    return (
        lax.broadcasted_iota(jnp.int32, (HALF, HALF), 0),
        lax.broadcasted_iota(jnp.int32, (HALF, HALF), 1),
    )


def pack_gram(gram, tiles):
    i, j = square_iota()
    low = gram[HALF:, HALF:]
    packed = (gram[:HALF, HALF:], jnp.where(i >= j, gram[:HALF, :HALF], low))
    diag = jnp.sum(jnp.where(i == j, low, 0.0), 0, keepdims=True)
    sub = lax.broadcasted_iota(jnp.int32, (8, HALF), 0)
    tail = jnp.where(sub == 4, diag, 0.0)
    for q in range(32):
        rows = packed[q // 16][8 * (q % 16) : 8 * (q % 16) + 8]
        tiles[2 * q] = jnp.where(sub < 4, rows, tail)
        tiles[2 * q + 1] = jnp.where(sub < 4, pltpu.roll(rows, 4, 0), tail)


def unpack_gram(rows, diag):
    i, j = square_iota()
    upper = jnp.concatenate(rows[:16], 0)
    both = jnp.concatenate(rows[16:], 0)
    flip = both.T
    first = jnp.where(i >= j, both, flip)
    second = jnp.where(i < j, both, jnp.where(i == j, diag, flip))
    return jnp.concatenate(
        [jnp.concatenate([first, upper], 1), jnp.concatenate([upper.T, second], 1)], 0
    )


def local_kernel(index, frames, row_factor, col_factor, slab_out, message, tiles):
    rows = row_factor[...].astype(F32)
    sums = []
    for b in range(frames.shape[0]):
        slab = jnp.dot(frames[b], col_factor[...], preferred_element_type=F32)
        slab_out[b] = slab
        sums.append(jnp.sum(slab * rows, 0, keepdims=True))
    pack_gram(inner_gram(col_factor[...]), tiles)
    own = tiles[index[0]]
    sums = jnp.concatenate([x[:, :HALF] for x in sums] + [x[:, HALF:] for x in sums], 0)
    for i in range(message.shape[0]):
        message[i, :8] = own
        message[i, 8:] = sums


def row_pack_kernel(factor, out):
    pack_gram(inner_gram(factor[...]), out)


def time_kernel(
    parts, row_parts, diags, time_gram, factor_out, time_out, inverse_out, col_gram
):
    sub = lax.broadcasted_iota(jnp.int32, (8, HALF), 0)
    row_rows, col_rows = [], []
    for q in range(32):
        even, odd = parts[2 * q], parts[2 * q + 1]
        row_rows.append(jnp.where(sub < 4, even, pltpu.roll(odd, 4, 0)))
        even = jnp.where(sub < 7, even, pltpu.roll(row_parts[2 * q], 2, 0))
        odd = jnp.where(sub < 7, odd, pltpu.roll(row_parts[2 * q + 1], 2, 0))
        col_rows.append(jnp.where(sub < 4, pltpu.roll(even, 4, 0), odd))
    col = unpack_gram(col_rows, diags[1:2, :])
    col_gram[...] = col
    inverse_out[...] = unpack_gram(row_rows, diags[0:1, :]) * col
    each = parts.shape[0] // 8
    rhs = [parts[each * i][7:8, :] for i in range(8)]
    rhs = jnp.concatenate(
        [jnp.concatenate(rhs[:4], 0), jnp.concatenate(rhs[4:], 0)], 1
    )

    @pl.loop(0, 4)
    def _(step):
        half_inverse(inverse_out)

        @pl.when(step == 1)
        def _():
            factor = matmul_f32(rhs, inverse_out[...])
            factor_out[...] = factor
            time_new = time_gram[...] + matmul_f32(factor, factor, ((0,), (0,)))
            time_out[...] = time_new
            inverse_out[...] = time_new * col_gram[...]


def split_gram(gram):
    high = gram.astype(jnp.bfloat16)
    return high, (gram - high.astype(F32)).astype(jnp.bfloat16)


def col_kernel(time_new, history, parts, out, inverse, sums):
    sub = lax.broadcasted_iota(jnp.int32, (8, R), 0)
    chunk = history.shape[0] // parts.shape[0]
    for q in range(32):
        rows = []
        for p in (2 * q, 2 * q + 1):
            part = parts[p].astype(F32)
            sums[chunk * p : chunk * p + chunk, :] = (
                history[chunk * p : chunk * p + chunk, :] + part[:chunk]
            )
            part = part[chunk:]
            rows.append(part + pltpu.roll(part, 4, 0))
        gram = jnp.where(sub < 4, rows[0], rows[1])
        inverse[8 * q : 8 * q + 8, :] = time_new[8 * q : 8 * q + 8, :] * gram

    @pl.loop(0, 2)
    def _(step):
        half_inverse(inverse)

    out[...] = matmul_f32(sums[...], inverse[...]).astype(out.dtype)


def gather(x, axis, count):
    return lax.all_to_all(jnp.broadcast_to(x[None], (count,) + x.shape), axis, 0, 0)


def body(frames, row_factor, col_factor, row_history, col_history, time_gram):
    nrow = lax.axis_size("row")
    ncol = lax.axis_size("col")
    nb = frames.shape[0]
    r = lax.axis_index("row")
    own = R // nrow
    square = jax.ShapeDtypeStruct((R, R), F32)
    tiles = jax.ShapeDtypeStruct((nrow, 8, HALF), F32)
    vmem = pl.BlockSpec(memory_space=pltpu.VMEM)
    slab_part, col_parts = pl.pallas_call(
        local_kernel,
        out_shape=(
            jax.ShapeDtypeStruct((nb,) + row_history.shape, F32),
            jax.ShapeDtypeStruct((ncol, 16, HALF), F32),
        ),
        in_specs=[pl.BlockSpec(memory_space=pltpu.SMEM), vmem, vmem, vmem],
        scratch_shapes=[pltpu.VMEM(tiles.shape, F32)],
        name="local_products",
    )(r.reshape(1), frames, row_factor, col_factor)
    slab_own = lax.psum_scatter(slab_part, "col", scatter_dimension=1, tiled=True)
    col_parts = lax.all_to_all(col_parts, "col", 0, 0).sum(0)
    row_tiles = pl.pallas_call(row_pack_kernel, out_shape=tiles, name="row_pack")(row_factor)
    sub = lax.broadcasted_iota(jnp.int32, tiles.shape, 1)
    rhs_rows = jnp.repeat(col_parts[8:], nrow // 8, axis=0)[:, None, :]
    row_tiles = jnp.where(
        sub < 5, row_tiles, jnp.where(sub == 5, col_parts[3][None, None], rhs_rows)
    )
    row_parts = lax.all_to_all(row_tiles, "row", 0, 0)
    row_own = row_parts.sum(0)
    message = jnp.concatenate([row_own[:4], col_parts[:3], row_own[6:7]], 0)
    diags = jnp.concatenate([row_own[4:5], col_parts[4:5], row_own[2:8]], 0)
    slab_own, message, diags = lax.optimization_barrier((slab_own, message, diags))
    parts = gather(message, "row", nrow)
    slab = lax.all_gather(slab_own, "col", axis=1, tiled=True)
    frame_factor, time_new, inverse = pl.pallas_call(
        time_kernel,
        out_shape=(jax.ShapeDtypeStruct((nb, R), F32), square, square),
        scratch_shapes=[pltpu.VMEM((R, R), F32)],
        name="time_solve",
    )(parts, row_parts, diags, time_gram)

    row_sums = row_history + jnp.sum(frame_factor[:, None, :] * slab, axis=0)
    new_row = matmul_f32(row_sums, inverse).astype(jnp.bfloat16)
    high, low = split_gram(inner_gram(new_row))
    products = jnp.einsum("bij,ir->bjr", frames, new_row, preferred_element_type=F32)
    col_part = jnp.sum(frame_factor[:, None, :] * products, axis=0)
    chunk = col_part.shape[0] // nrow
    message = jnp.concatenate(
        [
            col_part.astype(jnp.bfloat16).reshape(nrow, chunk, R),
            high.reshape(nrow, own, R),
            low.reshape(nrow, own, R),
        ],
        1,
    )
    total = lax.all_to_all(message, "row", 0, 0).astype(F32).sum(0)
    high, low = split_gram(total[chunk : chunk + own] + total[chunk + own :])
    total = jnp.concatenate([total[:chunk].astype(jnp.bfloat16), high, low], 0)
    new_col = pl.pallas_call(
        col_kernel,
        out_shape=jax.ShapeDtypeStruct(col_history.shape, jnp.bfloat16),
        scratch_shapes=[pltpu.VMEM((R, R), F32), pltpu.VMEM(col_history.shape, F32)],
        name="col_solve",
    )(time_new, col_history, gather(total, "row", nrow))
    return (frame_factor, new_row, new_col)


def solution(mesh):
    in_specs = (
        P(None, "row", "col"),
        P("row", None),
        P("col", None),
        P("row", None),
        P("col", None),
        P(),
    )
    out_specs = (P(), P("row", None), P("col", None))
    return jax.shard_map(body, mesh=mesh, in_specs=in_specs, out_specs=out_specs, check_vma=False)
```

```python
import jax
import jax.numpy as jnp
from jax import lax
from jax.experimental import pallas as pl
from jax.experimental.pallas import tpu as pltpu
from jax.sharding import PartitionSpec as P

R = 256
HALF = 128
HIGHEST = lax.Precision.HIGHEST
F32 = jnp.float32


def inner_gram(matrix):
    return lax.dot_general(
        matrix, matrix, (((0,), (0,)), ((), ())), preferred_element_type=F32
    )


def matmul_f32(a, b, dims=((1,), (0,))):
    return lax.dot_general(a, b, (dims, ((), ())), precision=HIGHEST, preferred_element_type=F32)


def eliminate8(tile, g):
    lane = lax.broadcasted_iota(jnp.int32, (8, R), 1)
    cols = [jnp.broadcast_to(tile[:, g + j : g + j + 1], (8, HALF)) for j in range(8)]
    s = {}
    for j in range(8):
        for i in range(j, 8):
            s[i, j] = s[j, i] = jnp.broadcast_to(cols[j][i : i + 1, :], (8, HALF))
    inside = (lane >= g) & (lane < g + 8)
    rows = []
    for i in range(8):
        row = jnp.broadcast_to(tile[i : i + 1, :], (8, R))
        rows.append(jnp.where(inside, jnp.where(lane == g + i, 1.0, 0.0), row))
    for k in range(8):
        inv = pl.reciprocal(s[k, k])
        p = {j: s[k, j] * inv for j in range(k + 1, 8)}
        rows[k] = rows[k] * jnp.concatenate([inv, inv], 1)
        new = {}
        for j in range(k + 1, 8):
            for i in range(8):
                if i == k or k < i < j:
                    continue
                new[i, j] = s[i, j] - s[i, k] * p[j]
        for i in range(8):
            if i != k:
                rows[i] = rows[i] - jnp.concatenate([s[i, k]] * 2, 1) * rows[k]
        for (i, j), v in new.items():
            s[i, j] = v
            if i > k:
                s[j, i] = v
        for j in range(k + 1, 8):
            s[k, j] = p[j]
    return rows


def half_inverse(m):
    lane8 = lax.broadcasted_iota(jnp.int32, (8, R), 1)
    sub8 = lax.broadcasted_iota(jnp.int32, (8, R), 0)
    groups = HALF // 8
    tiles = [m[8 * i : 8 * i + 8, :] for i in range(groups)]
    for b in range(groups):
        g = 8 * b
        rows = eliminate8(tiles[b], g)
        inside = (lane8 >= g) & (lane8 < g + 8)
        for i in list(range(b + 1, groups)) + list(range(b)):
            acc = [
                jnp.broadcast_to(tiles[i][:, g + j : g + j + 1], (8, R)) * rows[j]
                for j in range(8)
            ]
            while len(acc) > 1:
                acc = [acc[k] + acc[k + 1] for k in range(0, len(acc), 2)]
            tiles[i] = jnp.where(inside, 0.0, tiles[i]) - acc[0]
        merged = rows[0]
        for j in range(1, 8):
            merged = jnp.where(sub8 == j, rows[j], merged)
        tiles[b] = merged
    panel = jnp.concatenate(tiles, 0)
    rest = m[HALF:, :]
    update = matmul_f32(rest[:, :HALF], panel)
    m[:HALF, :HALF] = rest[:, HALF:] - update[:, HALF:]
    m[:HALF, HALF:] = -update[:, :HALF]
    m[HALF:, :HALF] = panel[:, HALF:]
    m[HALF:, HALF:] = panel[:, :HALF]


def invert(m):
    @pl.loop(0, 2)
    def _(step):
        half_inverse(m)


def square_iota():
    return (
        lax.broadcasted_iota(jnp.int32, (HALF, HALF), 0),
        lax.broadcasted_iota(jnp.int32, (HALF, HALF), 1),
    )


def pack_gram(gram, tiles):
    i, j = square_iota()
    low = gram[HALF:, HALF:]
    packed = (gram[:HALF, HALF:], jnp.where(i >= j, gram[:HALF, :HALF], low))
    diag = jnp.sum(jnp.where(i == j, low, 0.0), 0, keepdims=True)
    sub = lax.broadcasted_iota(jnp.int32, (8, HALF), 0)
    tail = jnp.where(sub == 4, diag, 0.0)
    for q in range(32):
        rows = packed[q // 16][8 * (q % 16) : 8 * (q % 16) + 8]
        tiles[2 * q] = jnp.where(sub < 4, rows, tail)
        tiles[2 * q + 1] = jnp.where(sub < 4, pltpu.roll(rows, 4, 0), tail)


def unpack_gram(rows, diag):
    i, j = square_iota()
    upper = jnp.concatenate(rows[:16], 0)
    both = jnp.concatenate(rows[16:], 0)
    flip = both.T
    first = jnp.where(i >= j, both, flip)
    second = jnp.where(i < j, both, jnp.where(i == j, diag, flip))
    return jnp.concatenate(
        [jnp.concatenate([first, upper], 1), jnp.concatenate([upper.T, second], 1)], 0
    )


def local_kernel(index, frames, row_factor, col_factor, slab_out, message, tiles):
    rows = row_factor[...].astype(F32)
    sums = []
    for b in range(frames.shape[0]):
        slab = jnp.dot(frames[b], col_factor[...], preferred_element_type=F32)
        slab_out[b] = slab
        sums.append(jnp.sum(slab * rows, 0, keepdims=True))
    pack_gram(inner_gram(col_factor[...]), tiles)
    own = tiles[index[0]]
    sums = jnp.concatenate([x[:, :HALF] for x in sums] + [x[:, HALF:] for x in sums], 0)
    for i in range(message.shape[0]):
        message[i, :8] = own
        message[i, 8:] = sums


def row_pack_kernel(factor, out):
    pack_gram(inner_gram(factor[...]), out)


def time_kernel(
    parts, row_parts, diags, time_gram, factor_out, time_out, system_out, col_gram, inverse
):
    sub = lax.broadcasted_iota(jnp.int32, (8, HALF), 0)
    row_rows, col_rows = [], []
    for q in range(32):
        even, odd = parts[2 * q], parts[2 * q + 1]
        row_rows.append(jnp.where(sub < 4, even, pltpu.roll(odd, 4, 0)))
        even = jnp.where(sub < 7, even, pltpu.roll(row_parts[2 * q], 2, 0))
        odd = jnp.where(sub < 7, odd, pltpu.roll(row_parts[2 * q + 1], 2, 0))
        col_rows.append(jnp.where(sub < 4, pltpu.roll(even, 4, 0), odd))
    col = unpack_gram(col_rows, diags[1:2, :])
    col_gram[...] = col
    inverse[...] = unpack_gram(row_rows, diags[0:1, :]) * col
    each = parts.shape[0] // 8
    rhs = [parts[each * i][7:8, :] for i in range(8)]
    rhs = jnp.concatenate(
        [jnp.concatenate(rhs[:4], 0), jnp.concatenate(rhs[4:], 0)], 1
    )

    invert(inverse)
    factor = matmul_f32(rhs, inverse[...])
    factor_out[...] = factor
    time_new = time_gram[...] + matmul_f32(factor, factor, ((0,), (0,)))
    time_out[...] = time_new
    system_out[...] = time_new * col_gram[...]


def inverse_kernel(system, inverse):
    inverse[...] = system[...]
    invert(inverse)


def split_gram(gram):
    high = gram.astype(jnp.bfloat16)
    return high, (gram - high.astype(F32)).astype(jnp.bfloat16)


def col_kernel(time_new, row_inverse, parts, inverse, gram):
    sub = lax.broadcasted_iota(jnp.int32, (8, R), 0)
    for q in range(32):
        rows = []
        for p in (2 * q, 2 * q + 1):
            part = parts[p].astype(F32)
            part = part[part.shape[0] - 8 :]
            rows.append(part + pltpu.roll(part, 4, 0))
        gram[8 * q : 8 * q + 8, :] = jnp.where(sub < 4, rows[0], rows[1])
    half = matmul_f32(gram[...], row_inverse[...])
    inverse[...] = time_new[...] * matmul_f32(row_inverse[...], half)
    invert(inverse)


def gather(x, axis, count):
    return lax.all_to_all(jnp.broadcast_to(x[None], (count,) + x.shape), axis, 0, 0)


def body(frames, row_factor, col_factor, row_history, col_history, time_gram):
    nrow = lax.axis_size("row")
    ncol = lax.axis_size("col")
    nb = frames.shape[0]
    r = lax.axis_index("row")
    own = R // nrow
    square = jax.ShapeDtypeStruct((R, R), F32)
    tiles = jax.ShapeDtypeStruct((nrow, 8, HALF), F32)
    vmem = pl.BlockSpec(memory_space=pltpu.VMEM)
    slab_part, col_parts = pl.pallas_call(
        local_kernel,
        out_shape=(
            jax.ShapeDtypeStruct((nb,) + row_history.shape, F32),
            jax.ShapeDtypeStruct((ncol, 16, HALF), F32),
        ),
        in_specs=[pl.BlockSpec(memory_space=pltpu.SMEM), vmem, vmem, vmem],
        scratch_shapes=[pltpu.VMEM(tiles.shape, F32)],
        name="local_products",
    )(r.reshape(1), frames, row_factor, col_factor)
    slab_own = lax.psum_scatter(slab_part, "col", scatter_dimension=1, tiled=True)
    col_parts = lax.all_to_all(col_parts, "col", 0, 0).sum(0)
    row_tiles = pl.pallas_call(row_pack_kernel, out_shape=tiles, name="row_pack")(row_factor)
    sub = lax.broadcasted_iota(jnp.int32, tiles.shape, 1)
    rhs_rows = jnp.repeat(col_parts[8:], nrow // 8, axis=0)[:, None, :]
    row_tiles = jnp.where(
        sub < 5, row_tiles, jnp.where(sub == 5, col_parts[3][None, None], rhs_rows)
    )
    row_parts = lax.all_to_all(row_tiles, "row", 0, 0)
    row_own = row_parts.sum(0)
    message = jnp.concatenate([row_own[:4], col_parts[:3], row_own[6:7]], 0)
    diags = jnp.concatenate([row_own[4:5], col_parts[4:5], row_own[2:8]], 0)
    slab_own, message, diags = lax.optimization_barrier((slab_own, message, diags))
    parts = gather(message, "row", nrow)
    slab = lax.all_gather(slab_own, "col", axis=1, tiled=True)
    frame_factor, time_new, system = pl.pallas_call(
        time_kernel,
        out_shape=(jax.ShapeDtypeStruct((nb, R), F32), square, square),
        scratch_shapes=[pltpu.VMEM((R, R), F32), pltpu.VMEM((R, R), F32)],
        name="frame_solve",
    )(parts, row_parts, diags, time_gram)

    row_sums = row_history + jnp.sum(frame_factor[:, None, :] * slab, axis=0)
    gram_part = matmul_f32(row_sums, row_sums, ((0,), (0,)))
    gram_part, system = lax.optimization_barrier((gram_part.reshape(nrow, own, R), system))
    gram_own = lax.all_to_all(gram_part, "row", 0, 0).sum(0)
    row_inverse = pl.pallas_call(inverse_kernel, out_shape=square, name="row_solve")(system)
    new_row = matmul_f32(row_sums, row_inverse).astype(jnp.bfloat16)
    products = jnp.einsum("bij,ir->bjr", frames, new_row, preferred_element_type=F32)
    col_part = jnp.sum(frame_factor[:, None, :] * products, axis=0)
    chunk = col_part.shape[0] // nrow
    halves = jnp.concatenate(split_gram(gram_own), 0)
    message = jnp.concatenate(
        [
            col_part.astype(jnp.bfloat16).reshape(nrow, chunk, R),
            jnp.broadcast_to(halves[None], (nrow,) + halves.shape),
        ],
        1,
    )
    received = lax.all_to_all(message, "row", 0, 0)
    total = received[:, :chunk].astype(F32).sum(0).astype(jnp.bfloat16)
    total = gather(total, "row", nrow).reshape(col_history.shape)
    col_inverse = pl.pallas_call(
        col_kernel,
        out_shape=square,
        scratch_shapes=[pltpu.VMEM((R, R), F32)],
        name="col_solve",
    )(time_new, row_inverse, received)
    new_col = matmul_f32(col_history + total.astype(F32), col_inverse).astype(jnp.bfloat16)
    return (frame_factor, new_row, new_col)


def solution(mesh):
    in_specs = (
        P(None, "row", "col"),
        P("row", None),
        P("col", None),
        P("row", None),
        P("col", None),
        P(),
    )
    out_specs = (P(), P("row", None), P("col", None))
    return jax.shard_map(body, mesh=mesh, in_specs=in_specs, out_specs=out_specs, check_vma=False)
```

```python
import jax
import jax.numpy as jnp
from jax import lax
from jax.experimental import pallas as pl
from jax.experimental.pallas import tpu as pltpu
from jax.sharding import PartitionSpec as P

R = 256
HALF = 128
HIGHEST = lax.Precision.HIGHEST
F32 = jnp.float32


def inner_gram(matrix):
    return lax.dot_general(
        matrix, matrix, (((0,), (0,)), ((), ())), preferred_element_type=F32
    )


def matmul_f32(a, b, dims=((1,), (0,))):
    return lax.dot_general(a, b, (dims, ((), ())), precision=HIGHEST, preferred_element_type=F32)


def eliminate8(tile, g):
    lane = lax.broadcasted_iota(jnp.int32, (8, R), 1)
    cols = [jnp.broadcast_to(tile[:, g + j : g + j + 1], (8, HALF)) for j in range(8)]
    s = {}
    for j in range(8):
        for i in range(j, 8):
            s[i, j] = s[j, i] = jnp.broadcast_to(cols[j][i : i + 1, :], (8, HALF))
    inside = (lane >= g) & (lane < g + 8)
    rows = []
    for i in range(8):
        row = jnp.broadcast_to(tile[i : i + 1, :], (8, R))
        rows.append(jnp.where(inside, jnp.where(lane == g + i, 1.0, 0.0), row))
    for k in range(8):
        inv = pl.reciprocal(s[k, k])
        p = {j: s[k, j] * inv for j in range(k + 1, 8)}
        rows[k] = rows[k] * jnp.concatenate([inv, inv], 1)
        new = {}
        for j in range(k + 1, 8):
            for i in range(8):
                if i == k or k < i < j:
                    continue
                new[i, j] = s[i, j] - s[i, k] * p[j]
        for i in range(8):
            if i != k:
                rows[i] = rows[i] - jnp.concatenate([s[i, k]] * 2, 1) * rows[k]
        for (i, j), v in new.items():
            s[i, j] = v
            if i > k:
                s[j, i] = v
        for j in range(k + 1, 8):
            s[k, j] = p[j]
    return rows


def half_inverse(m):
    lane8 = lax.broadcasted_iota(jnp.int32, (8, R), 1)
    sub8 = lax.broadcasted_iota(jnp.int32, (8, R), 0)
    groups = HALF // 8
    tiles = [m[8 * i : 8 * i + 8, :] for i in range(groups)]
    for b in range(groups):
        g = 8 * b
        rows = eliminate8(tiles[b], g)
        inside = (lane8 >= g) & (lane8 < g + 8)
        for i in list(range(b + 1, groups)) + list(range(b)):
            acc = [
                jnp.broadcast_to(tiles[i][:, g + j : g + j + 1], (8, R)) * rows[j]
                for j in range(8)
            ]
            new = jnp.where(inside, 0.0, tiles[i])
            for term in acc:
                new = new - term
            tiles[i] = new
        merged = rows[0]
        for j in range(1, 8):
            merged = jnp.where(sub8 == j, rows[j], merged)
        tiles[b] = merged
    panel = jnp.concatenate(tiles, 0)
    rest = m[HALF:, :]
    update = matmul_f32(rest[:, :HALF], panel)
    m[:HALF, :HALF] = rest[:, HALF:] - update[:, HALF:]
    m[:HALF, HALF:] = -update[:, :HALF]
    m[HALF:, :HALF] = panel[:, HALF:]
    m[HALF:, HALF:] = panel[:, :HALF]


def square_iota():
    return (
        lax.broadcasted_iota(jnp.int32, (HALF, HALF), 0),
        lax.broadcasted_iota(jnp.int32, (HALF, HALF), 1),
    )


def pack_gram(gram, tiles):
    i, j = square_iota()
    low = gram[HALF:, HALF:]
    packed = (gram[:HALF, HALF:], jnp.where(i >= j, gram[:HALF, :HALF], low))
    diag = jnp.sum(jnp.where(i == j, low, 0.0), 0, keepdims=True)
    sub = lax.broadcasted_iota(jnp.int32, (8, HALF), 0)
    tail = jnp.where(sub == 4, diag, 0.0)
    for q in range(32):
        rows = packed[q // 16][8 * (q % 16) : 8 * (q % 16) + 8]
        tiles[2 * q] = jnp.where(sub < 4, rows, tail)
        tiles[2 * q + 1] = jnp.where(sub < 4, pltpu.roll(rows, 4, 0), tail)


def unpack_gram(rows, diag):
    i, j = square_iota()
    upper = jnp.concatenate(rows[:16], 0)
    both = jnp.concatenate(rows[16:], 0)
    flip = both.T
    first = jnp.where(i >= j, both, flip)
    second = jnp.where(i < j, both, jnp.where(i == j, diag, flip))
    return jnp.concatenate(
        [jnp.concatenate([first, upper], 1), jnp.concatenate([upper.T, second], 1)], 0
    )


def local_kernel(index, frames, row_factor, col_factor, slab_out, message, tiles):
    rows = row_factor[...].astype(F32)
    sums = []
    for b in range(frames.shape[0]):
        slab = jnp.dot(frames[b], col_factor[...], preferred_element_type=F32)
        slab_out[b] = slab
        sums.append(jnp.sum(slab * rows, 0, keepdims=True))
    pack_gram(inner_gram(col_factor[...]), tiles)
    own = tiles[index[0]]
    sums = jnp.concatenate([x[:, :HALF] for x in sums] + [x[:, HALF:] for x in sums], 0)
    for i in range(message.shape[0]):
        message[i, :8] = own
        message[i, 8:] = sums


def row_pack_kernel(factor, out):
    pack_gram(inner_gram(factor[...]), out)


def time_kernel(
    parts, row_parts, diags, time_gram, factor_out, time_out, inverse_out, col_gram
):
    sub = lax.broadcasted_iota(jnp.int32, (8, HALF), 0)
    row_rows, col_rows = [], []
    for q in range(32):
        even, odd = parts[2 * q], parts[2 * q + 1]
        row_rows.append(jnp.where(sub < 4, even, pltpu.roll(odd, 4, 0)))
        even = jnp.where(sub < 7, even, pltpu.roll(row_parts[2 * q], 2, 0))
        odd = jnp.where(sub < 7, odd, pltpu.roll(row_parts[2 * q + 1], 2, 0))
        col_rows.append(jnp.where(sub < 4, pltpu.roll(even, 4, 0), odd))
    col = unpack_gram(col_rows, diags[1:2, :])
    col_gram[...] = col
    inverse_out[...] = unpack_gram(row_rows, diags[0:1, :]) * col
    each = parts.shape[0] // 8
    rhs = [parts[each * i][7:8, :] for i in range(8)]
    rhs = jnp.concatenate(
        [jnp.concatenate(rhs[:4], 0), jnp.concatenate(rhs[4:], 0)], 1
    )

    @pl.loop(0, 4)
    def _(step):
        half_inverse(inverse_out)

        @pl.when(step == 1)
        def _():
            factor = matmul_f32(rhs, inverse_out[...])
            factor_out[...] = factor
            time_new = time_gram[...] + matmul_f32(factor, factor, ((0,), (0,)))
            time_out[...] = time_new
            inverse_out[...] = time_new * col_gram[...]


def split_gram(gram):
    high = gram.astype(jnp.bfloat16)
    return high, (gram - high.astype(F32)).astype(jnp.bfloat16)


def col_kernel(time_new, history, parts, out, inverse, sums, past, loaded):
    sub = lax.broadcasted_iota(jnp.int32, (8, R), 0)
    chunk = history.shape[0] // parts.shape[0]
    load = pltpu.make_async_copy(history, past, loaded)
    load.start()
    for q in range(32):
        rows = []
        for p in (2 * q, 2 * q + 1):
            part = parts[p].astype(F32)
            sums[chunk * p : chunk * p + chunk, :] = part[:chunk]
            part = part[chunk:]
            rows.append(part + pltpu.roll(part, 4, 0))
        gram = jnp.where(sub < 4, rows[0], rows[1])
        inverse[8 * q : 8 * q + 8, :] = time_new[8 * q : 8 * q + 8, :] * gram

    @pl.loop(0, 2)
    def _(step):
        half_inverse(inverse)

    load.wait()
    out[...] = matmul_f32(past[...] + sums[...], inverse[...]).astype(out.dtype)


def gather(x, axis, count):
    return lax.all_to_all(jnp.broadcast_to(x[None], (count,) + x.shape), axis, 0, 0)


def body(frames, row_factor, col_factor, row_history, col_history, time_gram):
    nrow = lax.axis_size("row")
    ncol = lax.axis_size("col")
    nb = frames.shape[0]
    r = lax.axis_index("row")
    own = R // nrow
    square = jax.ShapeDtypeStruct((R, R), F32)
    tiles = jax.ShapeDtypeStruct((nrow, 8, HALF), F32)
    vmem = pl.BlockSpec(memory_space=pltpu.VMEM)
    slab_part, col_parts = pl.pallas_call(
        local_kernel,
        out_shape=(
            jax.ShapeDtypeStruct((nb,) + row_history.shape, F32),
            jax.ShapeDtypeStruct((ncol, 16, HALF), F32),
        ),
        in_specs=[pl.BlockSpec(memory_space=pltpu.SMEM), vmem, vmem, vmem],
        scratch_shapes=[pltpu.VMEM(tiles.shape, F32)],
        name="local_products",
    )(r.reshape(1), frames, row_factor, col_factor)
    slab_own = lax.psum_scatter(slab_part, "col", scatter_dimension=1, tiled=True)
    col_parts = lax.all_to_all(col_parts, "col", 0, 0).sum(0)
    row_tiles = pl.pallas_call(row_pack_kernel, out_shape=tiles, name="row_pack")(row_factor)
    sub = lax.broadcasted_iota(jnp.int32, tiles.shape, 1)
    rhs_rows = jnp.repeat(col_parts[8:], nrow // 8, axis=0)[:, None, :]
    row_tiles = jnp.where(
        sub < 5, row_tiles, jnp.where(sub == 5, col_parts[3][None, None], rhs_rows)
    )
    col_share, col_diag = col_parts[:3], col_parts[4:5]
    row_tiles, col_share, col_diag = lax.optimization_barrier((row_tiles, col_share, col_diag))
    row_parts = lax.all_to_all(row_tiles, "row", 0, 0)
    row_own = row_parts.sum(0)
    message = jnp.concatenate([row_own[:4], col_share, row_own[6:7]], 0)
    diags = jnp.concatenate([row_own[4:5], col_diag, row_own[2:8]], 0)
    slab_own, message, diags = lax.optimization_barrier((slab_own, message, diags))
    parts = gather(message, "row", nrow)
    slab = lax.all_gather(slab_own, "col", axis=1, tiled=True)
    frame_factor, time_new, inverse = pl.pallas_call(
        time_kernel,
        out_shape=(jax.ShapeDtypeStruct((nb, R), F32), square, square),
        scratch_shapes=[pltpu.VMEM((R, R), F32)],
        name="time_solve",
    )(parts, row_parts, diags, time_gram)

    row_sums = row_history + jnp.sum(frame_factor[:, None, :] * slab, axis=0)
    new_row = matmul_f32(row_sums, inverse).astype(jnp.bfloat16)
    high, low = split_gram(inner_gram(new_row))
    products = jnp.einsum("bij,ir->bjr", frames, new_row, preferred_element_type=F32)
    col_part = jnp.sum(frame_factor[:, None, :] * products, axis=0)
    chunk = col_part.shape[0] // nrow
    message = jnp.concatenate(
        [
            col_part.astype(jnp.bfloat16).reshape(nrow, chunk, R),
            high.reshape(nrow, own, R),
            low.reshape(nrow, own, R),
        ],
        1,
    )
    total = lax.all_to_all(message, "row", 0, 0).astype(F32).sum(0)
    high, low = split_gram(total[chunk : chunk + own] + total[chunk + own :])
    total = jnp.concatenate([total[:chunk].astype(jnp.bfloat16), high, low], 0)
    new_col = pl.pallas_call(
        col_kernel,
        out_shape=jax.ShapeDtypeStruct(col_history.shape, jnp.bfloat16),
        in_specs=[vmem, pl.BlockSpec(memory_space=pl.ANY), vmem],
        scratch_shapes=[
            pltpu.VMEM((R, R), F32),
            pltpu.VMEM(col_history.shape, F32),
            pltpu.VMEM(col_history.shape, F32),
            pltpu.SemaphoreType.DMA,
        ],
        name="col_solve",
    )(time_new, col_history, gather(total, "row", nrow))
    return (frame_factor, new_row, new_col)


def solution(mesh):
    in_specs = (
        P(None, "row", "col"),
        P("row", None),
        P("col", None),
        P("row", None),
        P("col", None),
        P(),
    )
    out_specs = (P(), P("row", None), P("col", None))
    return jax.shard_map(body, mesh=mesh, in_specs=in_specs, out_specs=out_specs, check_vma=False)
```

```python
import jax
import jax.numpy as jnp
from jax import lax
from jax.experimental import pallas as pl
from jax.experimental.pallas import tpu as pltpu
from jax.sharding import PartitionSpec as P

R = 256
HALF = 128
HIGHEST = lax.Precision.HIGHEST
F32 = jnp.float32


def inner_gram(matrix):
    return lax.dot_general(
        matrix, matrix, (((0,), (0,)), ((), ())), preferred_element_type=F32
    )


def matmul_f32(a, b, dims=((1,), (0,))):
    return lax.dot_general(a, b, (dims, ((), ())), precision=HIGHEST, preferred_element_type=F32)


def eliminate8(tile, g):
    lane = lax.broadcasted_iota(jnp.int32, (8, R), 1)
    cols = [jnp.broadcast_to(tile[:, g + j : g + j + 1], (8, HALF)) for j in range(8)]
    s = {}
    for j in range(8):
        for i in range(j, 8):
            s[i, j] = s[j, i] = jnp.broadcast_to(cols[j][i : i + 1, :], (8, HALF))
    inside = (lane >= g) & (lane < g + 8)
    rows = []
    for i in range(8):
        row = jnp.broadcast_to(tile[i : i + 1, :], (8, R))
        rows.append(jnp.where(inside, jnp.where(lane == g + i, 1.0, 0.0), row))
    for k in range(8):
        inv = pl.reciprocal(s[k, k])
        p = {j: s[k, j] * inv for j in range(k + 1, 8)}
        rows[k] = rows[k] * jnp.concatenate([inv, inv], 1)
        new = {}
        for j in range(k + 1, 8):
            for i in range(8):
                if i == k or k < i < j:
                    continue
                new[i, j] = s[i, j] - s[i, k] * p[j]
        for i in range(8):
            if i != k:
                rows[i] = rows[i] - jnp.concatenate([s[i, k]] * 2, 1) * rows[k]
        for (i, j), v in new.items():
            s[i, j] = v
            if i > k:
                s[j, i] = v
        for j in range(k + 1, 8):
            s[k, j] = p[j]
    return rows


def half_inverse(m):
    lane8 = lax.broadcasted_iota(jnp.int32, (8, R), 1)
    sub8 = lax.broadcasted_iota(jnp.int32, (8, R), 0)
    groups = HALF // 8
    tiles = [m[8 * i : 8 * i + 8, :] for i in range(groups)]
    for b in range(groups):
        g = 8 * b
        rows = eliminate8(tiles[b], g)
        inside = (lane8 >= g) & (lane8 < g + 8)
        for i in list(range(b + 1, groups)) + list(range(b)):
            acc = [
                jnp.broadcast_to(tiles[i][:, g + j : g + j + 1], (8, R)) * rows[j]
                for j in range(8)
            ]
            new = jnp.where(inside, 0.0, tiles[i])
            for term in acc:
                new = new - term
            tiles[i] = new
        merged = rows[0]
        for j in range(1, 8):
            merged = jnp.where(sub8 == j, rows[j], merged)
        tiles[b] = merged
    panel = jnp.concatenate(tiles, 0)
    rest = m[HALF:, :]
    update = matmul_f32(rest[:, :HALF], panel)
    m[:HALF, :HALF] = rest[:, HALF:] - update[:, HALF:]
    m[:HALF, HALF:] = -update[:, :HALF]
    m[HALF:, :HALF] = panel[:, HALF:]
    m[HALF:, HALF:] = panel[:, :HALF]


def square_iota():
    return (
        lax.broadcasted_iota(jnp.int32, (HALF, HALF), 0),
        lax.broadcasted_iota(jnp.int32, (HALF, HALF), 1),
    )


def pack_gram(gram, tiles):
    i, j = square_iota()
    low = gram[HALF:, HALF:]
    packed = (gram[:HALF, HALF:], jnp.where(i >= j, gram[:HALF, :HALF], low))
    diag = jnp.sum(jnp.where(i == j, low, 0.0), 0, keepdims=True)
    sub = lax.broadcasted_iota(jnp.int32, (8, HALF), 0)
    tail = jnp.where(sub == 4, diag, 0.0)
    for q in range(32):
        rows = packed[q // 16][8 * (q % 16) : 8 * (q % 16) + 8]
        tiles[2 * q] = jnp.where(sub < 4, rows, tail)
        tiles[2 * q + 1] = jnp.where(sub < 4, pltpu.roll(rows, 4, 0), tail)


def unpack_gram(rows, diag):
    i, j = square_iota()
    upper = jnp.concatenate(rows[:16], 0)
    both = jnp.concatenate(rows[16:], 0)
    flip = both.T
    first = jnp.where(i >= j, both, flip)
    second = jnp.where(i < j, both, jnp.where(i == j, diag, flip))
    return jnp.concatenate(
        [jnp.concatenate([first, upper], 1), jnp.concatenate([upper.T, second], 1)], 0
    )


def slab_kernel(frames, row_factor, col_factor, slab_out, sums_out):
    rows = row_factor[...].astype(F32)
    for b in range(frames.shape[0]):
        slab = jnp.dot(frames[b], col_factor[...], preferred_element_type=F32)
        slab_out[b] = slab
        total = jnp.sum(slab * rows, 0, keepdims=True)
        sums_out[b : b + 1, :] = total[:, :HALF]
        sums_out[b + 4 : b + 5, :] = total[:, HALF:]


def col_message_kernel(index, col_factor, sums, message, tiles):
    pack_gram(inner_gram(col_factor[...]), tiles)
    own = tiles[index[0]]
    for i in range(message.shape[0]):
        message[i, :8] = own
        message[i, 8:] = sums[...]


def row_pack_kernel(factor, out):
    pack_gram(inner_gram(factor[...]), out)


def time_kernel(
    parts, row_parts, diags, time_gram, factor_out, time_out, inverse_out, col_gram
):
    sub = lax.broadcasted_iota(jnp.int32, (8, HALF), 0)
    row_rows, col_rows = [], []
    for q in range(32):
        even, odd = parts[2 * q], parts[2 * q + 1]
        row_rows.append(jnp.where(sub < 4, even, pltpu.roll(odd, 4, 0)))
        even = jnp.where(sub < 7, even, pltpu.roll(row_parts[2 * q], 2, 0))
        odd = jnp.where(sub < 7, odd, pltpu.roll(row_parts[2 * q + 1], 2, 0))
        col_rows.append(jnp.where(sub < 4, pltpu.roll(even, 4, 0), odd))
    col = unpack_gram(col_rows, diags[1:2, :])
    col_gram[...] = col
    inverse_out[...] = unpack_gram(row_rows, diags[0:1, :]) * col
    each = parts.shape[0] // 8
    rhs = [parts[each * i][7:8, :] for i in range(8)]
    rhs = jnp.concatenate(
        [jnp.concatenate(rhs[:4], 0), jnp.concatenate(rhs[4:], 0)], 1
    )

    @pl.loop(0, 4)
    def _(step):
        half_inverse(inverse_out)

        @pl.when(step == 1)
        def _():
            factor = matmul_f32(rhs, inverse_out[...])
            factor_out[...] = factor
            time_new = time_gram[...] + matmul_f32(factor, factor, ((0,), (0,)))
            time_out[...] = time_new
            inverse_out[...] = time_new * col_gram[...]


def split_gram(gram):
    high = gram.astype(jnp.bfloat16)
    return high, (gram - high.astype(F32)).astype(jnp.bfloat16)


def col_kernel(time_new, history, parts, out, inverse, sums, past, loaded):
    sub = lax.broadcasted_iota(jnp.int32, (8, R), 0)
    chunk = history.shape[0] // parts.shape[0]
    load = pltpu.make_async_copy(history, past, loaded)
    load.start()
    for q in range(32):
        rows = []
        for p in (2 * q, 2 * q + 1):
            part = parts[p].astype(F32)
            sums[chunk * p : chunk * p + chunk, :] = part[:chunk]
            part = part[chunk:]
            rows.append(part + pltpu.roll(part, 4, 0))
        gram = jnp.where(sub < 4, rows[0], rows[1])
        inverse[8 * q : 8 * q + 8, :] = time_new[8 * q : 8 * q + 8, :] * gram

    @pl.loop(0, 2)
    def _(step):
        half_inverse(inverse)

    load.wait()
    out[...] = matmul_f32(past[...] + sums[...], inverse[...]).astype(out.dtype)


def gather(x, axis, count):
    return lax.all_to_all(jnp.broadcast_to(x[None], (count,) + x.shape), axis, 0, 0)


def body(frames, row_factor, col_factor, row_history, col_history, time_gram):
    nrow = lax.axis_size("row")
    ncol = lax.axis_size("col")
    nb = frames.shape[0]
    r = lax.axis_index("row")
    own = R // nrow
    square = jax.ShapeDtypeStruct((R, R), F32)
    tiles = jax.ShapeDtypeStruct((nrow, 8, HALF), F32)
    vmem = pl.BlockSpec(memory_space=pltpu.VMEM)
    slab_part, rhs_part = pl.pallas_call(
        slab_kernel,
        out_shape=(
            jax.ShapeDtypeStruct((nb,) + row_history.shape, F32),
            jax.ShapeDtypeStruct((8, HALF), F32),
        ),
        name="slab_products",
    )(frames, row_factor, col_factor)
    col_parts = pl.pallas_call(
        col_message_kernel,
        out_shape=jax.ShapeDtypeStruct((ncol, 16, HALF), F32),
        in_specs=[pl.BlockSpec(memory_space=pltpu.SMEM), vmem, vmem],
        scratch_shapes=[pltpu.VMEM(tiles.shape, F32)],
        name="col_message",
    )(r.reshape(1), col_factor, rhs_part)
    slab_own = lax.psum_scatter(slab_part, "col", scatter_dimension=1, tiled=True)
    col_parts = lax.all_to_all(col_parts, "col", 0, 0).sum(0)
    row_tiles = pl.pallas_call(row_pack_kernel, out_shape=tiles, name="row_pack")(row_factor)
    sub = lax.broadcasted_iota(jnp.int32, tiles.shape, 1)
    rhs_rows = jnp.repeat(col_parts[8:], nrow // 8, axis=0)[:, None, :]
    row_tiles = jnp.where(
        sub < 5, row_tiles, jnp.where(sub == 5, col_parts[3][None, None], rhs_rows)
    )
    col_share, col_diag = col_parts[:3], col_parts[4:5]
    row_tiles, col_share, col_diag = lax.optimization_barrier((row_tiles, col_share, col_diag))
    row_parts = lax.all_to_all(row_tiles, "row", 0, 0)
    row_own = row_parts.sum(0)
    message = jnp.concatenate([row_own[:4], col_share, row_own[6:7]], 0)
    diags = jnp.concatenate([row_own[4:5], col_diag, row_own[2:8]], 0)
    slab_own, message, diags = lax.optimization_barrier((slab_own, message, diags))
    parts = gather(message, "row", nrow)
    slab = lax.all_gather(slab_own, "col", axis=1, tiled=True)
    frame_factor, time_new, inverse = pl.pallas_call(
        time_kernel,
        out_shape=(jax.ShapeDtypeStruct((nb, R), F32), square, square),
        scratch_shapes=[pltpu.VMEM((R, R), F32)],
        name="time_solve",
    )(parts, row_parts, diags, time_gram)

    row_sums = row_history + jnp.sum(frame_factor[:, None, :] * slab, axis=0)
    new_row = matmul_f32(row_sums, inverse).astype(jnp.bfloat16)
    high, low = split_gram(inner_gram(new_row))
    products = jnp.einsum("bij,ir->bjr", frames, new_row, preferred_element_type=F32)
    col_part = jnp.sum(frame_factor[:, None, :] * products, axis=0)
    chunk = col_part.shape[0] // nrow
    message = jnp.concatenate(
        [
            col_part.astype(jnp.bfloat16).reshape(nrow, chunk, R),
            high.reshape(nrow, own, R),
            low.reshape(nrow, own, R),
        ],
        1,
    )
    total = lax.all_to_all(message, "row", 0, 0).astype(F32).sum(0)
    high, low = split_gram(total[chunk : chunk + own] + total[chunk + own :])
    total = jnp.concatenate([total[:chunk].astype(jnp.bfloat16), high, low], 0)
    new_col = pl.pallas_call(
        col_kernel,
        out_shape=jax.ShapeDtypeStruct(col_history.shape, jnp.bfloat16),
        in_specs=[vmem, pl.BlockSpec(memory_space=pl.ANY), vmem],
        scratch_shapes=[
            pltpu.VMEM((R, R), F32),
            pltpu.VMEM(col_history.shape, F32),
            pltpu.VMEM(col_history.shape, F32),
            pltpu.SemaphoreType.DMA,
        ],
        name="col_solve",
    )(time_new, col_history, gather(total, "row", nrow))
    return (frame_factor, new_row, new_col)


def solution(mesh):
    in_specs = (
        P(None, "row", "col"),
        P("row", None),
        P("col", None),
        P("row", None),
        P("col", None),
        P(),
    )
    out_specs = (P(), P("row", None), P("col", None))
    return jax.shard_map(body, mesh=mesh, in_specs=in_specs, out_specs=out_specs, check_vma=False)
```
